32 devices in a mesh: ctx: 2 (over x), group: 4 (over z), replica: 4 (over y, core).
Axes of the slice: x: 2, y: 2, z: 4, core: 2. Of those that a mesh axis runs over, the one named last changes fastest.
Arguments:
- patches: bfloat16 [16, 2048, 768], P(('group', 'replica'), 'ctx'), may hold values from -6 to 6
- cotangent: bfloat16 [16, 2048, 768], P(('group', 'replica'), 'ctx'), may hold values from -6 to 6
- qkv_weight: bfloat16 [768, 2304], P('group'), may hold values from -0.21875 to 0.21875
- qkv_bias: bfloat16 [2304], P('group'), may hold values from -3 to 3
- query_gain: bfloat16 [64], P('group'), may hold values from 0.099609375 to 1.8984375
- query_shift: bfloat16 [64], P('group'), may hold values from -3 to 3
- key_gain: bfloat16 [64], P('group'), may hold values from 0.099609375 to 1.8984375
- norm_gain: bfloat16 [768], P('group'), may hold values from 0.099609375 to 1.8984375
- norm_shift: bfloat16 [768], P('group'), may hold values from -3 to 3
- out_weight: bfloat16 [768, 768], P('group'), may hold values from -1.25 to 1.25
- out_bias: bfloat16 [768], P('group'), may hold values from -3 to 3
- mlp_gain: bfloat16 [768], P('group'), may hold values from 0.099609375 to 1.8984375
- mlp_shift: bfloat16 [768], P('group'), may hold values from -3 to 3
- up_weight: bfloat16 [768, 3072], P('group'), may hold values from -0.21875 to 0.21875
- up_bias: bfloat16 [3072], P('group'), may hold values from -3 to 3
- down_weight: bfloat16 [3072, 768], P('group'), may hold values from -0.109375 to 0.109375
- down_bias: bfloat16 [768], P('group'), may hold values from -3 to 3
Outputs:
- layer_out: bfloat16 [16, 2048, 768], P(('group', 'replica'), 'ctx')
- grad_patches: float32 [16, 2048, 768], P(('group', 'replica'), 'ctx')
- grad_qkv_weight: float32 [768, 2304], P('group')
- grad_qkv_bias: float32 [2304], P('group')
- grad_query_gain: float32 [64], P('group')
- grad_query_shift: float32 [64], P('group')
- grad_key_gain: float32 [64], P('group')
- grad_norm_gain: float32 [768], P('group')
- grad_norm_shift: float32 [768], P('group')
- grad_out_weight: float32 [768, 768], P('group')
- grad_out_bias: float32 [768], P('group')
- grad_mlp_gain: float32 [768], P('group')
- grad_mlp_shift: float32 [768], P('group')
- grad_up_weight: float32 [768, 3072], P('group')
- grad_up_bias: float32 [3072], P('group')
- grad_down_weight: float32 [3072, 768], P('group')
- grad_down_bias: float32 [768], P('group')
The draws below stay inside these ranges and needn't reach their ends.
All inputs are finite; a program needn't handle non-finite values.
Results may differ from the reference program's by a relative error of at most 0.019.
Values may be sent and summed in bfloat16 or wider, within the bound.
No kernel may reach another device: no remote copies, remote signals or barrier semaphores. Data moves between devices by JAX's collectives and lax.ppermute only.
A program may use at most 384 MiB of HBM per device.

```python
import jax
import jax.numpy as jnp
from jax import lax

D = 768
HEADS = 12
HEAD = 64
FF = 3072
SEQ = 2048
IMAGES = 16


def block_levels(rng, extent, shards, low, high):
    factor_of, own = 1.0, jax.random.fold_in(rng, 6)
    for axis_at, parts in shards:
        heights = jnp.exp(jax.random.uniform(jax.random.fold_in(own, axis_at), (parts,), jnp.float32, low / len(shards), high / len(shards)))
        factor_of = factor_of * jnp.repeat(heights, extent[axis_at] // parts).reshape([-1 if axis == axis_at else 1 for axis in range(len(extent))])
    return factor_of


def gaussian(stream_key, dims, width, most, pieces=(), held_as=jnp.bfloat16):
    level = block_levels(stream_key, dims, pieces, -0.22, 0.18) if pieces else 1.0
    result = jax.random.normal(stream_key, dims, jnp.float32) * width * level
    return jnp.minimum(jnp.maximum(result, -most), most).astype(held_as)


def setup_inputs(seed: int = 0) -> dict:
    key_of = jax.random.split(jax.random.key(seed), 18)
    return {
        "patches": gaussian(key_of[0], (IMAGES, SEQ, D), 1.0, 6.0, ((0, 16), (1, 2))),
        "cotangent": gaussian(key_of[1], (IMAGES, SEQ, D), 1.0, 6.0, ((0, 16), (1, 2))),
        "qkv_weight": gaussian(key_of[2], (D, 3 * D), D ** -0.5, 0.21875, ((0, 4),)),
        "qkv_bias": gaussian(key_of[3], (3 * D,), 0.5, 3.0, ((0, 4),)),
        "query_gain": jnp.clip(1.0 + 0.18 * jax.random.normal(key_of[4], (HEAD,), jnp.float32), 0.099609375, 1.8984375).astype(jnp.bfloat16),
        "query_shift": gaussian(key_of[5], (HEAD,), 0.5, 3.0, ((0, 4),)),
        "key_gain": jnp.clip(1.0 + 0.18 * jax.random.normal(key_of[6], (HEAD,), jnp.float32), 0.099609375, 1.8984375).astype(jnp.bfloat16),
        "norm_gain": jnp.clip(1.0 + 0.18 * jax.random.normal(key_of[7], (D,), jnp.float32), 0.099609375, 1.8984375).astype(jnp.bfloat16),
        "norm_shift": gaussian(key_of[8], (D,), 0.5, 3.0, ((0, 4),)),
        "out_weight": gaussian(key_of[9], (D, D), (D // 32) ** -0.5, 1.25, ((0, 4),)),
        "out_bias": gaussian(key_of[10], (D,), 0.5, 3.0, ((0, 4),)),
        "mlp_gain": jnp.clip(1.0 + 0.18 * jax.random.normal(key_of[11], (D,), jnp.float32), 0.099609375, 1.8984375).astype(jnp.bfloat16),
        "mlp_shift": gaussian(key_of[12], (D,), 0.5, 3.0, ((0, 4),)),
        "up_weight": gaussian(key_of[13], (D, FF), D ** -0.5, 0.21875, ((0, 4),)),
        "up_bias": gaussian(key_of[14], (FF,), 0.5, 3.0, ((0, 4),)),
        "down_weight": gaussian(key_of[15], (FF, D), FF ** -0.5, 0.109375, ((0, 4),)),
        "down_bias": gaussian(key_of[16], (D,), 0.5, 3.0, ((0, 4),)),
    }


@jax.custom_vjp
def low(v):
    return lax.optimization_barrier(v.astype(jnp.bfloat16)).astype(jnp.float32)

@jax.custom_vjp
def low_back(v):
    return v

def low_keep(v):
    return (low(v), None)

def low_pass(kept, grad):
    return (grad,)

def back_keep(v):
    return (v, None)

def back_low(kept, grad):
    return (low(grad),)
low.defvjp(low_keep, low_pass)
low_back.defvjp(back_keep, back_low)
EPS = 1e-06

def matmul(left, right):
    return jnp.dot(left, right, precision=lax.Precision.HIGHEST, preferred_element_type=jnp.float32)

def layer_norm(value, gain, shift):
    mean = lax.optimization_barrier(jnp.mean(value, -1, keepdims=True))
    cent = value - mean
    var = lax.optimization_barrier(jnp.mean(cent * cent, -1, keepdims=True))
    return cent * lax.rsqrt(var + EPS) * gain + shift

def gelu_tanh(value):
    coeff = (2.0 / jnp.pi) ** 0.5
    return 0.5 * value * (1.0 + jnp.tanh(coeff * (value + 0.044715 * value * value * value)))

def image_layer(params, image):
    qkv_weight, qkv_bias, query_gain, query_shift, key_gain, norm_gain, norm_shift, out_weight, out_bias, mlp_gain, mlp_shift, up_weight, up_bias, down_weight, down_bias = params
    hidden = low(layer_norm(image, norm_gain, norm_shift))
    qkv = low_back(matmul(hidden, qkv_weight) + qkv_bias)
    query = qkv[:, :D].reshape(SEQ, HEADS, HEAD)
    keys = qkv[:, D:2 * D].reshape(SEQ, HEADS, HEAD)
    values = low(qkv[:, 2 * D:].reshape(SEQ, HEADS, HEAD))
    query = low(layer_norm(query, query_gain, query_shift))
    keys = low(layer_norm(keys, key_gain, 0.0))
    scores = low_back(jnp.einsum('qhd,khd->hqk', query, keys, precision=lax.Precision.HIGHEST) * HEAD ** (-0.5))
    probs = low(jax.nn.softmax(scores, axis=-1))
    attn = jnp.einsum('hqk,khd->qhd', probs, values, precision=lax.Precision.HIGHEST).reshape(SEQ, D)
    attn = low_back(low(attn))
    branch = low_back(matmul(attn, out_weight) + out_bias)
    mixed = image + branch
    hidden_two = low(layer_norm(mixed, mlp_gain, mlp_shift))
    upper = low_back(matmul(hidden_two, up_weight) + up_bias)
    active = low(gelu_tanh(upper))
    return mixed + matmul(active, down_weight) + down_bias

def reference(patches, cotangent, qkv_weight, qkv_bias, query_gain, query_shift, key_gain, norm_gain, norm_shift, out_weight, out_bias, mlp_gain, mlp_shift, up_weight, up_bias, down_weight, down_bias):
    params = tuple((p.astype(jnp.float32) for p in (qkv_weight, qkv_bias, query_gain, query_shift, key_gain, norm_gain, norm_shift, out_weight, out_bias, mlp_gain, mlp_shift, up_weight, up_bias, down_weight, down_bias)))
    inputs = patches.astype(jnp.float32)

    def whole(images, weights):
        step = jax.checkpoint(lambda image: image_layer(weights, image))
        return lax.map(step, images)
    output, pull = jax.vjp(whole, inputs, params)
    grad_input, grad_params = pull(cotangent.astype(jnp.float32))
    return (output.astype(jnp.bfloat16), grad_input, grad_params[0], grad_params[1], grad_params[2], grad_params[3], grad_params[4], grad_params[5], grad_params[6], grad_params[7], grad_params[8], grad_params[9], grad_params[10], grad_params[11], grad_params[12], grad_params[13], grad_params[14])
```

```python
import functools

import jax
import jax.numpy as jnp
from jax import lax
from jax.experimental import pallas as pl
from jax.experimental.pallas import tpu as pltpu
from jax.sharding import PartitionSpec as P

HEADS = 12
HEAD = 64
EPS = 1e-06
BF = jnp.bfloat16
F32 = jnp.float32
NT = (((1,), (1,)), ((), ()))
LOG2E = 1.4426950408889634
LN2 = 0.6931471805599453
SHIFT = 10.0
ALPHA = LOG2E * HEAD ** (-0.5)
AUG = 16
QCH = 3
VMEM = pl.BlockSpec(memory_space=pltpu.VMEM)
SMEM = pl.BlockSpec(memory_space=pltpu.SMEM)
ANY = pl.BlockSpec(memory_space=pl.ANY)


def params(limit=62 * 2**20):
    return pltpu.CompilerParams(vmem_limit_bytes=limit)


def cost(flops, nbytes, trans=0):
    return pl.CostEstimate(flops=int(flops), bytes_accessed=int(nbytes), transcendentals=int(trans))


def dot(a, b):
    return jnp.dot(a, b, preferred_element_type=F32)


def dot_nt(a, b):
    return lax.dot_general(a, b, NT, preferred_element_type=F32)


def rows_norm(x):
    mean = jnp.mean(x, -1, keepdims=True)
    cent = x - mean
    rstd = lax.rsqrt(jnp.mean(cent * cent, -1, keepdims=True) + EPS)
    return cent * rstd, rstd


def rows_norm_back(grad, normed, rstd, gain):
    eg = grad * gain
    return (
        eg - jnp.mean(eg, -1, keepdims=True) - normed * jnp.mean(eg * normed, -1, keepdims=True)
    ) * rstd


def split3(row):
    hi = row.astype(BF)
    rest = row - hi.astype(F32)
    mid = rest.astype(BF)
    low = (rest - mid.astype(F32)).astype(BF)
    return hi.astype(F32), mid.astype(F32), low.astype(F32)


def aug_rows(row):
    hi, mid, low = split3(row)
    at = lax.broadcasted_iota(jnp.int32, (AUG, row.shape[1]), 0)
    out = jnp.where(at == 0, hi, jnp.where(at == 1, mid, jnp.where(at == 2, low, 0.0)))
    return out.astype(BF)


def ones_rows(n):
    at = lax.broadcasted_iota(jnp.int32, (AUG, n), 0)
    return jnp.where(at < 3, 1.0, 0.0).astype(BF)


class Plan:
    def __init__(self, mesh):
        self.X = mesh.shape["ctx"]
        self.G = mesh.shape["group"]
        self.R = mesh.shape["replica"]
        self.Y = self.R // 2
        self.fast = self.X == 2 and self.Y == 2 and (768 // self.G) % 64 == 0
        self.NXY = 4 if self.fast else 1
        self.zrows = 768 // self.G
        self.prow = self.zrows // self.NXY
        ff = 3072 // self.G
        self.NM = 2 if (ff // 2) % 128 == 0 and self.fast else 3
        self.SEG = ff // self.NM
        self.CH = 768 // self.SEG
        self.drow = self.SEG // self.NXY // 2
        self.upc = self.G // 2
        self.uprows = self.upc * self.prow
        self.mrows = self.uprows + self.CH * self.drow

    def perm(self, dx, dy, dc, dz):
        pairs = []
        for x in range(self.X):
            for z in range(self.G):
                for y in range(self.Y):
                    for c in range(2):
                        src = (x * self.G + z) * self.R + 2 * y + c
                        dst = ((x ^ dx) * self.G + (z + dz) % self.G) * self.R + 2 * (y ^ dy) + (c ^ dc)
                        pairs.append((src, dst))
        return pairs

    def send(self, v, dx=0, dy=0, dc=0, dz=0):
        return lax.ppermute(v, ("ctx", "group", "replica"), self.perm(dx, dy, dc, dz))

    def swap(self, v):
        pairs = []
        for z in range(self.G):
            for y in range(self.Y):
                a = z * self.R + 2 * y + 1
                b = (self.G + z) * self.R + 2 * y
                pairs += [(a, b), (b, a)]
        return lax.ppermute(v, ("ctx", "group", "replica"), pairs)


PLANE = ((0, 0), (0, 1), (1, 0), (1, 1))


def norm_in_kernel(own_ref, oth_ref, vec_ref, h_ref):
    gain, shift = vec_ref[0:1, :], vec_ref[1:2, :]
    rows = own_ref.shape[0]
    n, _ = rows_norm(own_ref[...].astype(F32))
    h_ref[pl.ds(0, rows), :] = (n * gain + shift).astype(BF)
    n, _ = rows_norm(oth_ref[...].astype(F32))
    h_ref[pl.ds(rows, rows), :] = (n * gain + shift).astype(BF)


def norm_in(own, oth, vec):
    rows, width = own.shape
    return pl.pallas_call(
        norm_in_kernel,
        in_specs=[VMEM] * 3,
        out_specs=VMEM,
        out_shape=jax.ShapeDtypeStruct((2 * rows, width), BF),
        compiler_params=params(),
        cost_estimate=cost(20 * 2 * rows * width, 8 * rows * width),
    )(own, oth, vec)


def load_rows(plan, sc_ref, stacks, dst_of, sem):
    copies = []
    for e, d, ref in stacks:
        for s in range(plan.G):
            copies += [
                pltpu.make_async_copy(src, dst, sem) for src, dst in dst_of(e, d, s, ref)
            ]
    for c in copies:
        c.start()
    return copies


def piece_at(plan, sc_ref, d, s, sign):
    xy = sc_ref[2] ^ d if plan.NXY > 1 else 0
    z = lax.rem(sc_ref[3] + (plan.G - s if sign < 0 else s), plan.G)
    return xy, z


def fwd_kernel(plan, chunk, sc_ref, h_ref, bias_ref, gains_ref, *refs):
    stacks = refs[: plan.NXY]
    q_out, k_out, v_out, nq_out, nk_out, r_out, own_out, oth_out, lo_out, w_ref = refs[plan.NXY : plan.NXY + 10]
    kn_ref, acc_ref, sem = refs[plan.NXY + 10 :]
    rows = h_ref.shape[0]

    def dst_of(e, d, s, ref):
        xy, z = piece_at(plan, sc_ref, d, s, -1)
        at = pl.multiple_of(z * plan.zrows + xy * plan.prow, 16)
        return [(ref.at[s], w_ref.at[pl.ds(at, plan.prow), :])]

    copies = load_rows(plan, sc_ref, [(0, d, stacks[d]) for d in range(plan.NXY)], dst_of, sem)
    for c in copies:
        c.wait()
    wt = w_ref[...].T
    ones = ones_rows(rows)
    at = lax.broadcasted_iota(jnp.int32, (AUG, rows), 0)
    minus = jnp.where(at == 0, -SHIFT, 0.0).astype(BF)
    for part in range(3):
        y = dot_nt(wt[128 * part : 128 * part + 128, :], h_ref[...])
        y = y + bias_ref[128 * part : 128 * part + 128, chunk : chunk + 1]
        for a in range(2):
            x = y[64 * a : 64 * a + 64, :]
            if part == 2:
                v_out[a, 0:64, :] = x.astype(BF)
                v_out[a, 64:80, :] = ones
                continue
            mean = jnp.mean(x, 0, keepdims=True)
            cent = x - mean
            rstd = lax.rsqrt(jnp.mean(cent * cent, 0, keepdims=True) + EPS)
            n = cent * rstd
            r_out[2 * part + a : 2 * part + a + 1, :] = rstd
            if part == 0:
                nq_out[64 * a : 64 * a + 64, :] = n.astype(BF)
                val = (n * gains_ref[:, 0:1] + gains_ref[:, 1:2]) * ALPHA
                q_out[a, 0:64, :] = val.astype(BF)
                q_out[a, 64:80, :] = minus
            else:
                nk_out[64 * a : 64 * a + 64, :] = n.astype(BF)
                k_out[a, 0:64, :] = (n * gains_ref[:, 2:3]).astype(BF)
                k_out[a, 64:80, :] = ones

    kb = 512
    half = rows // 2

    def head(a, _):
        kn_ref[...] = k_out[a].T
        acc = None
        for j in range(rows // kb):
            st = dot(kn_ref[j * kb : (j + 1) * kb, :], q_out[a])
            p = jnp.exp2(st).astype(BF)
            o = dot(v_out[a, :, j * kb : (j + 1) * kb], p)
            if j == 0:
                acc_ref[...] = o
            else:
                acc_ref[...] += o
        total = acc_ref[64:65, :]
        inv = 1.0 / total
        full = acc_ref[0:64, :] * inv
        o = full.astype(BF)
        at0 = pl.multiple_of(a * 64, 64)
        own_out[pl.ds(at0, 64), :] = o[:, :half]
        oth_out[pl.ds(at0, 64), :] = o[:, half:]
        lo_out[pl.ds(at0, 64), :] = (full - o.astype(F32)).astype(BF)
        q_out[a, 64:80, :] = aug_rows(-(SHIFT + jnp.log(total) * LOG2E))
        return 0

    lax.fori_loop(0, 2, head, 0)


def attend_fwd(plan, chunk, sc, h1, bias, gains, stacks):
    rows = h1.shape[0]
    sd = jax.ShapeDtypeStruct
    return pl.pallas_call(
        functools.partial(fwd_kernel, plan, chunk),
        in_specs=[SMEM, VMEM, VMEM, VMEM] + [ANY] * plan.NXY,
        out_specs=[VMEM] * 10,
        out_shape=[
            sd((2, 80, rows), BF),
            sd((2, 80, rows), BF),
            sd((2, 80, rows), BF),
            sd((128, rows), BF),
            sd((128, rows), BF),
            sd((8, rows), F32),
            sd((128, rows // 2), BF),
            sd((128, rows // 2), BF),
            sd((128, rows), BF),
            sd((768, 384), BF),
        ],
        scratch_shapes=[
            pltpu.VMEM((rows, 80), BF),
            pltpu.VMEM((80, rows), F32),
            pltpu.SemaphoreType.DMA,
        ],
        compiler_params=params(),
        cost_estimate=cost(16e9, 10e6, 8.4e6),
    )(sc, h1, bias, gains, *stacks)


def out_kernel(plan, sc_ref, pat_ref, vec_ref, *refs):
    at_refs = refs[:6]
    stacks = refs[6 : 6 + 2 * plan.NXY]
    x1_out, h2_out, w_ref = refs[6 + 2 * plan.NXY : 9 + 2 * plan.NXY]
    an_ref, sem = refs[9 + 2 * plan.NXY :]

    def dst_of(e, d, s, ref):
        xy, z = piece_at(plan, sc_ref, d, s, -1)
        at = pl.multiple_of(z * plan.zrows + xy * plan.prow, 16)
        return [(ref.at[s], w_ref.at[sc_ref[1] ^ e, pl.ds(at, plan.prow), :])]

    copies = load_rows(
        plan,
        sc_ref,
        [(e, d, stacks[e * plan.NXY + d]) for e in range(2) for d in range(plan.NXY)],
        dst_of,
        sem,
    )
    for m in range(6):
        off = (sc_ref[0] if m < 3 else 1 - sc_ref[0]) * 384 + (m % 3) * 128
        an_ref[:, pl.ds(pl.multiple_of(off, 128), 128)] = at_refs[m][...].T
    for c in copies:
        c.wait()
    for i in range(2):
        x1_out[:, 384 * i : 384 * i + 384] = (
            dot(an_ref[...], w_ref[i])
            + pat_ref[:, 384 * i : 384 * i + 384].astype(F32)
            + vec_ref[2:3, 384 * i : 384 * i + 384]
        )
    n, _ = rows_norm(x1_out[...])
    h2_out[...] = (n * vec_ref[3:4, :] + vec_ref[4:5, :]).astype(BF)


def out_proj(plan, sc, pat, vec, attn, stacks):
    rows, width = pat.shape
    sd = jax.ShapeDtypeStruct
    return pl.pallas_call(
        functools.partial(out_kernel, plan),
        in_specs=[SMEM, VMEM, VMEM] + [VMEM] * 6 + [ANY] * (2 * plan.NXY),
        out_specs=[VMEM] * 3,
        out_shape=[sd((rows, width), F32), sd((rows, width), BF), sd((2, 768, 384), BF)],
        scratch_shapes=[pltpu.VMEM((rows, 768), BF), pltpu.SemaphoreType.DMA],
        compiler_params=params(),
        cost_estimate=cost(2 * rows * 768 * 768, 12e6),
    )(sc, pat, vec, *attn, *stacks)


def gelu_parts(value):
    coeff = (2.0 / jnp.pi) ** 0.5
    sq = value * value
    tangent = jnp.tanh(coeff * value * (1.0 + 0.044715 * sq))
    half = 0.5 * (1.0 + tangent)
    slope = half + 0.5 * value * (1.0 - tangent * tangent) * (coeff * (1.0 + 3.0 * 0.044715 * sq))
    return value * half, slope


def mlp_kernel(plan, last, sc_ref, h_ref, g_ref, y_in, dh_in, bup_ref, vec_ref, *refs):
    stacks = refs[: 2 * plan.NXY]
    y_out, dh_out, sb_out, keep_ref, send_ref = refs[2 * plan.NXY : 2 * plan.NXY + 5]
    wu_ref, wd_ref, gu_ref, gd_ref, ht_ref, acc_ref, sem = refs[2 * plan.NXY + 5 :]
    G, SEG, CH = plan.G, plan.SEG, plan.CH

    def spots(e, d, s, ref, sign, up, down, c_at):
        xy, z = piece_at(plan, sc_ref, d, s, sign)
        cc = sc_ref[1] ^ e
        a0 = pl.multiple_of(z * plan.zrows + xy * plan.prow, 16)
        b0 = pl.multiple_of(z * SEG + (xy * 2 + cc) * plan.drow, 16)
        if plan.fast:
            yield up.at[pl.ds(cc * plan.upc, plan.upc), pl.ds(a0, plan.prow), :], slice(0, plan.upc)
            yield down.at[:, pl.ds(b0, plan.drow), :], slice(plan.upc, 2 * plan.upc)
            return
        for u in range(plan.upc):
            yield up.at[cc * plan.upc + u, pl.ds(a0, plan.prow), :], pl.ds(u * plan.prow, plan.prow)
        for v in range(CH):
            yield down.at[v, pl.ds(b0, plan.drow), :], pl.ds(plan.uprows + v * plan.drow, plan.drow)

    copies = []
    for e in range(2):
        for d in range(plan.NXY):
            ref = stacks[e * plan.NXY + d]
            for s in range(G):
                for spot, at in spots(e, d, s, ref, -1, wu_ref, wd_ref, None):
                    copies.append(pltpu.make_async_copy(ref.at[s, at], spot, sem))
    for c in copies:
        c.start()
    ht_ref[...] = h_ref[...].T
    for c in copies:
        c.wait()

    def seg(f, _):
        fs = pl.ds(pl.multiple_of(f * SEG, 128), SEG)
        u = dot(h_ref[...], wu_ref[f]) + bup_ref[pl.ds(f, 1), :]
        z, slope = gelu_parts(u)
        zb = z.astype(BF)
        dz = jnp.zeros(u.shape, F32)
        for v in range(CH):
            wd = wd_ref[v, fs, :]
            cs = slice(v * SEG, (v + 1) * SEG)
            dz = dz + dot_nt(g_ref[:, cs], wd)
            upd = dot(zb, wd)
            acc_ref[:, cs] += upd
        du = (dz * slope).astype(BF)
        zt = zb.T
        for v in range(CH):
            cs = slice(v * SEG, (v + 1) * SEG)
            gd_ref[v, fs, :] = dot(zt, g_ref[:, cs]).astype(BF)
        gu_ref[f] = dot(ht_ref[...], du).astype(BF)
        dh_out[...] += dot_nt(du, wu_ref[f])
        sb_out[pl.ds(f, 1), :] = jnp.sum(du.astype(F32), 0, keepdims=True)
        return 0

    acc_ref[...] = y_in[...]
    if dh_in is None:
        dh_out[...] = jnp.zeros(dh_out.shape, F32)
    else:
        dh_out[...] = dh_in[...]
    lax.fori_loop(0, G, seg, 0)
    outs = []
    for e in (1, 0):
        dst = send_ref if e else keep_ref
        for d in range(plan.NXY):
            for s in range(G):
                for spot, at in spots(e, d, s, None, 1, gu_ref, gd_ref, None):
                    outs.append(pltpu.make_async_copy(spot, dst.at[d, s, at], sem))
    for c in outs:
        c.start()
    if last:
        y_out[...] = (acc_ref[...] + vec_ref[5:6, :]).astype(BF)
    else:
        y_out[...] = acc_ref[...]
    for c in outs:
        c.wait()


def mlp_part(plan, last, sc, h2, g, y, dh, bup, vec, stacks):
    rows, width = h2.shape
    sd = jax.ShapeDtypeStruct
    first = dh is None

    def body(sc_ref, h_ref, g_ref, y_in, *rest):
        if first:
            return mlp_kernel(plan, last, sc_ref, h_ref, g_ref, y_in, None, *rest)
        return mlp_kernel(plan, last, sc_ref, h_ref, g_ref, y_in, *rest)

    piece = (2 * plan.upc, plan.prow, plan.SEG) if plan.fast else (plan.mrows, plan.SEG)
    ga = sd((plan.NXY, plan.G) + piece, BF)
    ffp = 3072 // plan.NM
    return pl.pallas_call(
        body,
        in_specs=[SMEM, VMEM, VMEM, VMEM] + ([] if first else [VMEM]) + [VMEM, VMEM] + [ANY] * (2 * plan.NXY),
        out_specs=[VMEM, VMEM, VMEM, ANY, ANY],
        out_shape=[
            sd((rows, width), BF if last else F32),
            sd((rows, width), F32),
            sd((plan.G, plan.SEG), F32),
            ga,
            ga,
        ],
        scratch_shapes=[
            pltpu.VMEM((plan.G, 768, plan.SEG), BF),
            pltpu.VMEM((plan.CH, ffp, plan.SEG), BF),
            pltpu.VMEM((plan.G, 768, plan.SEG), BF),
            pltpu.VMEM((plan.CH, ffp, plan.SEG), BF),
            pltpu.VMEM((768, rows), BF),
            pltpu.VMEM((rows, width), F32),
            pltpu.SemaphoreType.DMA,
        ],
        compiler_params=params(),
        cost_estimate=cost(12 * rows * 768 * ffp, 24e6, rows * ffp),
    )(sc, h2, g, y, *([] if first else [dh]), bup, vec, *stacks)


def mid_back_kernel(plan, sc_ref, x1_ref, dh_ref, g_ref, vec_ref, w_ref, *refs):
    at_refs = refs[:6]
    dx_out, sv_out, keep_ref, send_ref = refs[6:10]
    da_outs = refs[10:16]
    gw_ref, sem = refs[16:]
    dh = dh_ref[...]
    n, rstd = rows_norm(x1_ref[...])
    g = g_ref[...].astype(F32)
    dx = g + rows_norm_back(dh, n, rstd, vec_ref[3:4, :])
    dx_out[...] = dx
    da = dx.astype(BF)
    sv_out[...] = jnp.zeros(sv_out.shape, F32)
    sv_out[0:1, :] = jnp.sum(da.astype(F32), 0, keepdims=True)
    sv_out[1:2, :] = jnp.sum(dh * n, 0, keepdims=True)
    sv_out[2:3, :] = jnp.sum(dh, 0, keepdims=True)
    sv_out[3:4, :] = jnp.sum(g, 0, keepdims=True)
    for m in range(6):
        off = (sc_ref[0] if m < 3 else 1 - sc_ref[0]) * 384 + (m % 3) * 128
        rs = pl.ds(pl.multiple_of(off, 128), 128)
        da_outs[m][...] = (
            dot_nt(w_ref[0, rs, :], da[:, :384]) + dot_nt(w_ref[1, rs, :], da[:, 384:])
        ).astype(BF)
        for i in range(2):
            gw_ref[i, rs, :] = dot(at_refs[m][...], da[:, 384 * i : 384 * i + 384]).astype(BF)
    outs = []
    for e in (1, 0):
        dst = send_ref if e else keep_ref
        for d in range(plan.NXY):
            for s in range(plan.G):
                xy, z = piece_at(plan, sc_ref, d, s, 1)
                at = pl.multiple_of(z * plan.zrows + xy * plan.prow, 16)
                outs.append(
                    pltpu.make_async_copy(
                        gw_ref.at[sc_ref[1] ^ e, pl.ds(at, plan.prow), :], dst.at[d, s], sem
                    )
                )
    for c in outs:
        c.start()
    for c in outs:
        c.wait()


def mid_back(plan, sc, x1, dh2, g, vec, wout, attn):
    rows, width = x1.shape
    sd = jax.ShapeDtypeStruct
    ga = sd((plan.NXY, plan.G, plan.prow, 384), BF)
    return pl.pallas_call(
        functools.partial(mid_back_kernel, plan),
        in_specs=[SMEM] + [VMEM] * 5 + [VMEM] * 6,
        out_specs=[VMEM, VMEM, ANY, ANY] + [VMEM] * 6,
        out_shape=[sd((rows, width), F32), sd((8, width), F32), ga, ga] + [sd((128, rows), BF)] * 6,
        scratch_shapes=[pltpu.VMEM((2, 768, 384), BF), pltpu.SemaphoreType.DMA],
        compiler_params=params(),
        cost_estimate=cost(4 * rows * 768 * 768, 20e6),
    )(sc, x1, dh2, g, vec, wout, *attn)


def bwd_kernel(plan, sc_ref, h_ref, q_ref, k_ref, v_ref, nq_ref, nk_ref, r_ref, own_ref, oth_ref, lo_ref, do_own, do_oth, gains_ref, *refs):
    dqkv_out, ga_ref, sb_out, sg_out = refs[:4]
    qn_ref, kn_ref, dn_ref, dt_ref, dq_ref, dk_ref, dv_ref, gw_ref, sem = refs[4:]
    rows = h_ref.shape[0]
    half = rows // 2
    qb = kb = 512
    sg_out[...] = jnp.zeros(sg_out.shape, F32)

    def head(a, _):
        at0 = pl.ds(pl.multiple_of(a * 64, 64), 64)
        for t, (o_ref, d_ref) in enumerate(((own_ref, do_own), (oth_ref, do_oth))):
            ls = slice(t * half, (t + 1) * half)
            do = d_ref[at0, :]
            o = o_ref[at0, :].astype(F32) + lo_ref[at0, ls].astype(F32)
            dsum = jnp.sum(do.astype(F32) * o, 0, keepdims=True)
            dt_ref[0:64, ls] = do
            dt_ref[64:80, ls] = aug_rows(-dsum)
        qn_ref[...] = q_ref[a].T
        kn_ref[...] = k_ref[a].T
        dn_ref[...] = dt_ref[...].T

        for i in range(rows // qb):
            rs = slice(i * qb, (i + 1) * qb)
            dq = None
            for j in range(rows // kb):
                ks = slice(j * kb, (j + 1) * kb)
                p = jnp.exp2(dot(qn_ref[rs, :], k_ref[a, :, ks]))
                dp = dot(dn_ref[rs, :], v_ref[a, :, ks])
                ds = (p * dp).astype(BF)
                t = dot(ds, kn_ref[ks, :])
                dq = t if dq is None else dq + t
                tv = dot(dt_ref[0:64, rs], p.astype(BF))
                tk = dot(q_ref[a, 0:64, rs], ds)
                if i == 0:
                    dv_ref[:, ks] = tv
                    dk_ref[:, ks] = tk
                else:
                    dv_ref[:, ks] += tv
                    dk_ref[:, ks] += tk
            dq_ref[:, rs] = dq.T[:64]

        def norm_back(e, n, rstd, gain):
            eg = e * gain
            return rstd * (
                eg - jnp.mean(eg, 0, keepdims=True) - n * jnp.mean(eg * n, 0, keepdims=True)
            )

        e = dq_ref[...] * HEAD ** (-0.5)
        n = nq_ref[at0, :].astype(F32)
        dqkv_out[at0, :] = norm_back(e, n, r_ref[pl.ds(a, 1), :], gains_ref[:, 0:1]).astype(BF)
        sg_out[:, 0:1] += jnp.sum(e * n, 1, keepdims=True)
        sg_out[:, 1:2] += jnp.sum(e, 1, keepdims=True)
        e = dk_ref[...] * LN2
        n = nk_ref[at0, :].astype(F32)
        dqkv_out[pl.ds(pl.multiple_of(128 + a * 64, 64), 64), :] = norm_back(
            e, n, r_ref[pl.ds(2 + a, 1), :], gains_ref[:, 2:3]
        ).astype(BF)
        sg_out[:, 2:3] += jnp.sum(e * n, 1, keepdims=True)
        dqkv_out[pl.ds(pl.multiple_of(256 + a * 64, 64), 64), :] = dv_ref[...].astype(BF)
        return 0

    lax.fori_loop(0, 2, head, 0)
    gw_ref[...] = dot(dqkv_out[...], h_ref[...]).T.astype(BF)
    outs = []
    for d in range(plan.NXY):
        for s in range(plan.G):
            xy, z = piece_at(plan, sc_ref, d, s, 1)
            at = pl.multiple_of(z * plan.zrows + xy * plan.prow, 16)
            outs.append(
                pltpu.make_async_copy(gw_ref.at[pl.ds(at, plan.prow), :], ga_ref.at[d, s], sem)
            )
    for c in outs:
        c.start()
    sb_out[...] = jnp.broadcast_to(
        jnp.sum(dqkv_out[...].astype(F32), 1, keepdims=True), sb_out.shape
    )
    for c in outs:
        c.wait()


def attend_bwd(plan, sc, h1, saved, do_own, do_oth, gains):
    rows = h1.shape[0]
    sd = jax.ShapeDtypeStruct
    return pl.pallas_call(
        functools.partial(bwd_kernel, plan),
        in_specs=[SMEM] + [VMEM] * 13,
        out_specs=[VMEM, ANY, VMEM, VMEM],
        out_shape=[
            sd((384, rows), BF),
            sd((plan.NXY, plan.G, plan.prow, 384), BF),
            sd((384, 128), F32),
            sd((64, 128), F32),
        ],
        scratch_shapes=[
            pltpu.VMEM((rows, 80), BF),
            pltpu.VMEM((rows, 80), BF),
            pltpu.VMEM((rows, 80), BF),
            pltpu.VMEM((80, rows), BF),
            pltpu.VMEM((64, rows), F32),
            pltpu.VMEM((64, rows), F32),
            pltpu.VMEM((64, rows), F32),
            pltpu.VMEM((768, 384), BF),
            pltpu.SemaphoreType.DMA,
        ],
        compiler_params=params(),
        cost_estimate=cost(40e9, 12e6, 8.4e6),
    )(sc, h1, *saved, do_own, do_oth, gains)


def dh_oth_kernel(*refs):
    dq, w, out_ref = refs[:QCH], refs[QCH : 2 * QCH], refs[-1]
    half = out_ref.shape[0]
    acc = None
    for j in range(QCH):
        t = dot_nt(dq[j][:, half:].T, w[j][...])
        acc = t if acc is None else acc + t
    out_ref[...] = acc.astype(BF)


def dh_oth(dqkv, w):
    rows = dqkv[0].shape[1]
    return pl.pallas_call(
        dh_oth_kernel,
        in_specs=[VMEM] * (2 * QCH),
        out_specs=VMEM,
        out_shape=jax.ShapeDtypeStruct((rows // 2, 768), BF),
        compiler_params=params(),
        cost_estimate=cost(rows * 768 * 1152, 8e6),
    )(*dqkv, *w)


def dh_own_kernel(rcv_ref, pat_ref, dx_ref, vec_ref, *refs):
    dq, w = refs[:QCH], refs[QCH : 2 * QCH]
    out_ref, low_ref, sv_out = refs[2 * QCH :]
    half = out_ref.shape[0]
    dh = rcv_ref[...].astype(F32)
    for j in range(QCH):
        dh = dh + dot_nt(dq[j][:, :half].T, w[j][...])
    n, rstd = rows_norm(pat_ref[...].astype(F32))
    out = dx_ref[...] + rows_norm_back(dh, n, rstd, vec_ref[0:1, :])
    out_ref[...] = out
    low_ref[...] = out.astype(BF)
    sv_out[...] = jnp.zeros(sv_out.shape, F32)
    sv_out[0:1, :] = jnp.sum(dh * n, 0, keepdims=True)
    sv_out[1:2, :] = jnp.sum(dh, 0, keepdims=True)


def dh_own(rcv, pat, dx, vec, dqkv, w):
    rows, width = pat.shape
    sd = jax.ShapeDtypeStruct
    return pl.pallas_call(
        dh_own_kernel,
        in_specs=[VMEM] * (4 + 2 * QCH),
        out_specs=[VMEM] * 3,
        out_shape=[sd((rows, width), F32), sd((rows, width), BF), sd((8, width), F32)],
        compiler_params=params(),
        cost_estimate=cost(2 * rows * 768 * 1152, 20e6),
    )(rcv, pat, dx, vec, *dqkv, *w)


def add_kernel(n, *refs):
    ins, outs = refs[:n], refs[n:]
    for k, out in enumerate(outs):
        acc = ins[0][k].astype(F32)
        for r in ins[1:]:
            acc = acc + r[k].astype(F32)
        out[...] = acc.astype(out.dtype)


def add_split(arrays):
    shape = arrays[0].shape
    n = len(arrays)
    size = 2 * arrays[0].size
    return pl.pallas_call(
        functools.partial(add_kernel, n),
        in_specs=[VMEM] * n,
        out_specs=[VMEM] * shape[0],
        out_shape=[jax.ShapeDtypeStruct(shape[1:], BF)] * shape[0],
        compiler_params=params(),
        cost_estimate=cost(n * arrays[0].size, (n + 1) * size),
    )(*arrays)


def gather_pieces(plan, piece, cores):
    if not plan.fast:
        both = piece if cores else piece[None]
        every = lax.all_gather(both, "group", axis=0)
        every = jnp.stack([every[(-s) % plan.G] for s in range(plan.G)])
        return [every[:, i] for i in range(both.shape[0])]
    got = [piece] + [plan.send(piece, dz=s) for s in range(1, plan.G)]
    stack = jnp.stack(got)
    plane = [stack] + [plan.send(stack, dx=dx, dy=dy) for dx, dy in PLANE[1:]]
    if cores:
        plane = plane + [plan.send(v, dc=1) for v in plane]
    return plane


def reduce_pieces(plan, keep, send):
    cores = send is not None
    if not plan.fast:
        if cores:
            both = jnp.stack([keep[0], send[0]])
        else:
            c = lax.axis_index("replica") % 2
            zero = jnp.zeros_like(keep[0])
            both = jnp.where(c == 0, jnp.stack([keep[0], zero]), jnp.stack([zero, keep[0]]))
        mine = lax.psum_scatter(both, "group", scatter_dimension=1, tiled=True)
        mine = lax.psum(mine, ("ctx", "replica"))
        return [mine[0, 0], mine[1, 0]]
    if cores:
        parts = add_split([keep, plan.send(send, dc=1)])
    else:
        parts = [keep[i] for i in range(4)]
    arrived = [parts[0]] + [plan.send(parts[i], dx=dx, dy=dy) for i, (dx, dy) in enumerate(PLANE) if i]
    parts = add_split(arrived)
    arrived = [parts[0]] + [plan.send(parts[s], dz=s) for s in range(1, plan.G)]
    total = add_split([a[None] for a in arrived])[0]
    plane = [total] + [plan.send(total, dx=dx, dy=dy) for dx, dy in PLANE[1:]]
    return plane + [plan.send(v, dc=1) for v in plane]


def per_device(plan, *args):
    (
        patches, cotangent, wqkv, bqkv, qgain, qshift, kgain, gain1, shift1, wout, bout,
        gain2, shift2, wup, bup, wdown, bdown,
    ) = args
    G, SEG, NM, NXY = plan.G, plan.SEG, plan.NM, plan.NXY
    images, local, width = patches.shape
    x = lax.axis_index("ctx")
    z = lax.axis_index("group")
    r = lax.axis_index("replica")
    y, c = r // 2, r % 2
    zero = jnp.zeros((), jnp.int32)
    fast = plan.fast
    sc = jnp.stack([c, c if fast else zero, 2 * x + y if fast else zero, z if fast else zero]).astype(jnp.int32)
    stay = x == c

    pat0 = patches.reshape(local, width)
    cot0 = cotangent.reshape(local, width)
    pat = jnp.where(stay, pat0, plan.swap(pat0))
    pat_oth = plan.send(pat, dc=1)

    small = jnp.concatenate(
        [
            jnp.stack([gain1, shift1, bout, gain2, shift2, bdown]).reshape(-1),
            bup.reshape(-1),
            bqkv.reshape(-1),
            qgain,
            qshift,
            kgain,
        ]
    )
    got = [small] + [plan.send(small, dz=s) for s in range(1, G)]
    stackd = jnp.stack(got)
    every = jnp.take(stackd, (z - jnp.arange(G)) % G, axis=0).astype(F32)
    zr = plan.zrows
    vec = every[:, : 6 * zr].reshape(G, 6, zr).transpose(1, 0, 2).reshape(6, 768)
    vec = jnp.concatenate([vec, jnp.zeros((2, 768), F32)])
    at = 6 * zr
    ffz = 3072 // G
    bup_all = every[:, at : at + ffz].reshape(G, NM, SEG)
    at += ffz
    bq_all = every[:, at : at + 3 * zr].reshape(3, 2, QCH, 128)
    at += 3 * zr
    bias = lax.dynamic_index_in_dim(bq_all, c, 1, False).transpose(0, 2, 1).reshape(384, QCH)
    bias = jnp.pad(bias, ((0, 0), (0, 128 - QCH)))
    gains = every[:, at:].reshape(G, 3, HEAD // G).transpose(0, 2, 1).reshape(HEAD, 3)
    gains = jnp.pad(gains, ((0, 0), (0, 125)))

    pr = plan.prow
    xy = sc[2]

    def rows_of(v, n):
        return lax.dynamic_slice_in_dim(v, xy * n, n, 0)

    wq = rows_of(wqkv, pr).reshape(pr, 3, 2, QCH, 128)
    wq = lax.dynamic_index_in_dim(wq, c, 2, False)
    qpieces = [wq[:, :, j].reshape(pr, 384) for j in range(QCH)]
    qst = [gather_pieces(plan, p, False) for p in qpieces]

    wo = rows_of(wout, pr).reshape(pr, 2, 384).transpose(1, 0, 2)
    wu = rows_of(wup, pr).reshape(pr, G, NM, SEG)
    wd = wdown.reshape(NM, NXY, 2, plan.drow, plan.CH, SEG)
    wd = lax.dynamic_index_in_dim(wd, xy, 1, False)

    def own_core(v):
        return lax.dynamic_index_in_dim(v, c, 0, False) if fast else v

    wo = own_core(wo)

    def mpiece(t):
        up = wu[:, :, t].reshape(pr, 2, plan.upc, SEG).transpose(1, 2, 0, 3)
        down = wd[t].transpose(0, 2, 1, 3)
        if not fast:
            up, down = up.reshape(2, -1, SEG), down.reshape(2, -1, SEG)
        return own_core(jnp.concatenate([up, down], 1))

    mpieces = [mpiece(t) for t in range(NM)]
    ost = gather_pieces(plan, wo, True)
    mst = [gather_pieces(plan, p, True) for p in mpieces]

    cot = jnp.where(stay, cot0, plan.swap(cot0))

    h1 = norm_in(pat, pat_oth, vec)
    saved, own_o, oth_o, wqs = [], [], [], []
    for j in range(QCH):
        *keep, own, oth, low, w = attend_fwd(plan, j, sc, h1, bias, gains, qst[j])
        saved.append((*keep, own, oth, low))
        own_o.append(own)
        oth_o.append(plan.send(oth, dc=1))
        wqs.append(w)
    attn = own_o + oth_o
    x1, h2, wo_full = out_proj(plan, sc, pat, vec, attn, ost)
    yv, dh2 = x1, None
    sbs, mgrads = [], []
    for t in range(NM):
        yv, dh2, sb, keep, send = mlp_part(
            plan, t == NM - 1, sc, h2, cot, yv, dh2, bup_all[:, t], vec, mst[t]
        )
        sbs.append(sb)
        mgrads.append(reduce_pieces(plan, keep, send))
    layer_out = jnp.where(stay, yv, plan.swap(yv))

    dx1, sv3, okeep, osend, *dattn = mid_back(plan, sc, x1, dh2, cot, vec, wo_full, attn)
    ograd = reduce_pieces(plan, okeep, osend)
    dqkv, qgrads, sbq, sgq = [], [], [], []
    for j in range(QCH):
        far = plan.send(dattn[QCH + j], dc=1)
        d, ga, sb, sg = attend_bwd(plan, sc, h1, saved[j], dattn[j], far, gains)
        dqkv.append(d)
        qgrads.append(reduce_pieces(plan, ga, None))
        sbq.append(sb)
        sgq.append(sg)
    rcv = plan.send(dh_oth(dqkv, wqs), dc=1)
    gp, gp_low, sv1 = dh_own(rcv, pat, dx1, vec, dqkv, wqs)
    grad_patches = jnp.where(stay, gp, plan.swap(gp_low).astype(F32))

    def place(pieces, rows):
        if not fast:
            return jnp.stack([p[None] for p in pieces])
        st = jnp.stack(pieces).reshape((2, 4) + pieces[0].shape)
        order = xy ^ jnp.arange(4)
        st = jnp.take(st, order, axis=1)
        return jnp.where(c == 0, st, st[::-1])

    og = place(ograd, pr)
    g_wout = og.transpose(1, 2, 0, 3).reshape(zr, 768).astype(F32)
    ups, downs = [], []
    for t in range(NM):
        mg = place(mgrads[t], pr)
        if not fast:
            mg = mg.reshape(2, NXY, -1, pr, SEG)
        ups.append(mg[:, :, : plan.upc].transpose(1, 3, 0, 2, 4).reshape(zr, G, SEG))
        dn = mg[:, :, plan.upc :].reshape(2, NXY, plan.CH, plan.drow, SEG)
        downs.append(dn.transpose(1, 0, 3, 2, 4).reshape(SEG, 768))
    g_wup = jnp.stack(ups, 2).reshape(zr, 3072).astype(F32)
    g_wdown = jnp.concatenate(downs, 0).astype(F32)
    qg = jnp.stack([place(qgrads[j], pr) for j in range(QCH)])
    g_wqkv = qg.reshape(QCH, 2, zr, 3, 128).transpose(2, 3, 1, 0, 4).reshape(zr, 2304).astype(F32)

    bq = jnp.stack([s[:, 0] for s in sbq])
    bq = bq.reshape(QCH, 3, 128).transpose(1, 0, 2)
    zq = jnp.zeros_like(bq)
    bq = jnp.where(c == 0, jnp.stack([bq, zq], 1), jnp.stack([zq, bq], 1)).reshape(2304)
    sg = sgq[0][:, :3] + sgq[1][:, :3] + sgq[2][:, :3]
    sb = jnp.stack(sbs, 1).reshape(3072)
    v6 = jnp.concatenate([sv1[:2], sv3[:4]])
    pack = jnp.concatenate(
        [
            v6.reshape(6, G, zr).transpose(1, 0, 2).reshape(G, -1),
            sb.reshape(G, -1),
            bq.reshape(G, -1),
            sg.reshape(G, HEAD // G, 3).transpose(0, 2, 1).reshape(G, -1),
        ],
        1,
    )
    total = pack
    if fast:
        rest = [plan.send(pack, dx=dx, dy=dy, dc=dc) for dx, dy in PLANE for dc in range(2) if dx or dy or dc]
        for v in rest:
            total = total + v
        mine = lax.dynamic_index_in_dim(total, z, 0, False)
        for s in range(1, G):
            v = lax.dynamic_index_in_dim(total, (z + s) % G, 0, False)
            mine = mine + plan.send(v, dz=s)
    else:
        mine = lax.psum(total, ("ctx", "replica"))
        mine = lax.psum_scatter(mine, "group", scatter_dimension=0, tiled=True)[0]
    s6 = mine[: 6 * zr].reshape(6, zr)
    at = 6 * zr
    g_bup = mine[at : at + ffz]
    at += ffz
    g_bqkv = mine[at : at + 3 * zr]
    at += 3 * zr
    qk = mine[at:].reshape(3, HEAD // G)
    return (
        layer_out.reshape(images, local, width),
        grad_patches.reshape(images, local, width),
        g_wqkv,
        g_bqkv,
        qk[0],
        qk[1],
        qk[2],
        s6[0],
        s6[1],
        g_wout,
        s6[2],
        s6[3],
        s6[4],
        g_wup,
        g_bup,
        g_wdown,
        s6[5],
    )


def solution(mesh):
    plan = Plan(mesh)
    rows = P(("group", "replica"), "ctx", None)
    mat, vec = P("group", None), P("group")
    weights = (mat, vec, vec, vec, vec, vec, vec, mat, vec, vec, vec, mat, vec, mat, vec)
    return jax.shard_map(
        functools.partial(per_device, plan),
        mesh=mesh,
        in_specs=(rows, rows) + weights,
        out_specs=(rows, rows) + weights,
        check_vma=False,
    )
```
